32 devices in a mesh: seqhi: 8 (over y, x, core), seqlo: 4 (over z).
Axes of the slice: x: 2, y: 2, z: 4, core: 2. Of those that a mesh axis runs over, the one named last changes fastest.
Arguments:
- tokens: bfloat16 [32768, 768], P(('seqhi', 'seqlo')), may hold values from -6 to 6
- cotangent: bfloat16 [32768, 768], P(('seqhi', 'seqlo')), may hold values from -6 to 6
- first_kernel_weight: bfloat16 [2304, 384], replicated, may hold values from -0.125 to 0.125
- first_pointwise_weight: bfloat16 [768, 384], replicated, may hold values from -0.3125 to 0.3125
- second_kernel_weight: bfloat16 [2304, 384], replicated, may hold values from -0.125 to 0.125
- second_pointwise_weight: bfloat16 [768, 384], replicated, may hold values from -0.3125 to 0.3125
Outputs:
- output: bfloat16 [32768, 768], P(('seqhi', 'seqlo'))
- token_rows_gradient: bfloat16 [32768, 768], P(('seqhi', 'seqlo'))
- first_kernel_gradient: float32 [2304, 384], P(('seqhi', 'seqlo'))
- first_pointwise_gradient: float32 [768, 384], P(('seqhi', 'seqlo'))
- second_kernel_gradient: float32 [2304, 384], P(('seqhi', 'seqlo'))
- second_pointwise_gradient: float32 [768, 384], P(('seqhi', 'seqlo'))
The draws below stay inside these ranges and needn't reach their ends.
All inputs are finite; a program needn't handle non-finite values.
Results may differ from the reference program's by a relative error of at most 0.015.
Values may be sent and summed in bfloat16 or wider, within the bound.
A program may use at most 128 MiB of HBM per device.

```python
import jax
import jax.numpy as jnp

D = 768
H = 384
TAPS = 3
BINS = 32768
FIRST_SPACING = 4096
SECOND_SPACING = 8192


def with_spikes(drawn, key, source, target, parts, factor):
    owner, partner = [(jnp.arange(drawn.shape[dim]) // (drawn.shape[dim] // parts)).reshape([-1 if axis == dim else 1 for axis in range(drawn.ndim)]) for dim in (source, target)]
    chosen = jax.random.permutation(key, parts)[partner]
    strong = (owner == chosen) | (owner == (partner + parts // 2) % parts)
    return jnp.where(strong, factor * drawn, drawn)


def steps_of(stream_key, extent, cuts, least, high):
    factor_of, own = 1.0, jax.random.fold_in(stream_key, 6)
    for dim, blocks in cuts:
        steps = jnp.exp(jax.random.uniform(jax.random.fold_in(own, dim), (blocks,), jnp.float32, least / len(cuts), high / len(cuts)))
        factor_of = factor_of * jnp.repeat(steps, extent[dim] // blocks).reshape([-1 if axis == dim else 1 for axis in range(len(extent))])
    return factor_of


def bell_draw(stream_key, dims, width, limit, pieces=(), kind=jnp.bfloat16):
    factor_of = steps_of(stream_key, dims, pieces, -0.22, 0.18) if pieces else 1.0
    entries = jax.random.normal(stream_key, dims, jnp.float32) * width * factor_of
    return jnp.minimum(jnp.maximum(entries, -limit), limit).astype(kind)


def heavy_noise(rng, shape, width, reach, split, heavy, held_as=jnp.bfloat16):
    values = width * jax.random.normal(rng, shape, jnp.float32)
    if split:
        values = values * steps_of(rng, shape, split, -0.22, 0.18)
    return jnp.clip(with_spikes(values, jax.random.fold_in(rng, 3), *heavy), -reach, reach).astype(held_as)


def setup_inputs(seed: int = 0) -> dict:
    arg_keys = jax.random.split(jax.random.key(seed), 7)
    tokens = heavy_noise(arg_keys[0], (BINS, D), 1.0, 6.0, ((0, 32),), (0, 1, 32, 2.75))
    cotangent = heavy_noise(arg_keys[1], (BINS, D), 1.0, 6.0, ((0, 32),), (0, 1, 32, 2.75))
    first_kernel_weight = bell_draw(arg_keys[2], (TAPS * D, H), (TAPS * D) ** -0.5, 0.125)
    first_pointwise_weight = bell_draw(arg_keys[3], (D, H), H ** -0.5, 0.3125)
    second_kernel_weight = bell_draw(arg_keys[4], (TAPS * D, H), (TAPS * D) ** -0.5, 0.125)
    second_pointwise_weight = bell_draw(arg_keys[5], (D, H), H ** -0.5, 0.3125)
    return dict(tokens=tokens, cotangent=cotangent, first_kernel_weight=first_kernel_weight, first_pointwise_weight=first_pointwise_weight, second_kernel_weight=second_kernel_weight, second_pointwise_weight=second_pointwise_weight)


def shifted(values, offset):
    padding = jnp.zeros((abs(offset), values.shape[1]), values.dtype)
    if offset > 0:
        return jnp.concatenate([values[offset:], padding], 0)
    return jnp.concatenate([padding, values[:offset]], 0)

def tap_inputs(tokens, dilation):
    return (shifted(tokens, -dilation), tokens, shifted(tokens, dilation))

def residual_block_forward(tokens, conv_weight, proj_weight, dilation):
    tap_rows = tap_inputs(tokens, dilation)
    pre = jnp.zeros((tokens.shape[0], H), jnp.float32)
    for tap_index in range(TAPS):
        pre = pre + jnp.dot(tap_rows[tap_index], conv_weight[tap_index * D:(tap_index + 1) * D], preferred_element_type=jnp.float32)
    inner = jax.nn.gelu(pre).astype(jnp.bfloat16)
    result = (tokens.astype(jnp.float32) + jnp.dot(inner, proj_weight.T, preferred_element_type=jnp.float32)).astype(jnp.bfloat16)
    return (result, pre, inner)

def residual_block_backward(grad_out, tokens, pre, inner, conv_weight, proj_weight, dilation):
    grad_proj = jnp.dot(grad_out.T, inner, preferred_element_type=jnp.float32)
    grad_inner = jnp.dot(grad_out, proj_weight, preferred_element_type=jnp.float32)
    _, pullback = jax.vjp(jax.nn.gelu, pre)
    grad_pre = pullback(grad_inner)[0].astype(jnp.bfloat16)
    tap_rows = tap_inputs(tokens, dilation)
    grad_conv = jnp.concatenate([jnp.dot(tap_rows[tap_index].T, grad_pre, preferred_element_type=jnp.float32) for tap_index in range(TAPS)], 0)
    moved = (shifted(grad_pre, dilation), grad_pre, shifted(grad_pre, -dilation))
    grad_in = grad_out.astype(jnp.float32)
    for tap_index in range(TAPS):
        grad_in = grad_in + jnp.dot(moved[tap_index], conv_weight[tap_index * D:(tap_index + 1) * D].T, preferred_element_type=jnp.float32)
    return (grad_in.astype(jnp.bfloat16), grad_conv, grad_proj)

def reference(tokens, cotangent, first_kernel_weight, first_pointwise_weight, second_kernel_weight, second_pointwise_weight):
    between_blocks_state, first_preactivation, first_hidden_state = residual_block_forward(tokens, first_kernel_weight, first_pointwise_weight, FIRST_SPACING)
    output, second_preactivation, second_hidden_state = residual_block_forward(between_blocks_state, second_kernel_weight, second_pointwise_weight, SECOND_SPACING)
    between_blocks_gradient, second_kernel_gradient, second_pointwise_gradient = residual_block_backward(cotangent, between_blocks_state, second_preactivation, second_hidden_state, second_kernel_weight, second_pointwise_weight, SECOND_SPACING)
    token_rows_gradient, first_kernel_gradient, first_pointwise_gradient = residual_block_backward(between_blocks_gradient, tokens, first_preactivation, first_hidden_state, first_kernel_weight, first_pointwise_weight, FIRST_SPACING)
    return (output, token_rows_gradient, first_kernel_gradient, first_pointwise_gradient, second_kernel_gradient, second_pointwise_gradient)
```

```python
import jax
import jax.numpy as jnp
from jax import lax
from jax.sharding import PartitionSpec as P

FIRST_SPACING = 4096
SECOND_SPACING = 8192


def shifted(x, axis, by):
    devices = lax.axis_size(axis)
    pairs = [(i, i + by) for i in range(devices) if 0 <= i + by < devices]
    return lax.ppermute(x, axis, pairs)


def contract_rows(left, right):
    return lax.dot_general(
        left, right, (((0,), (0,)), ((), ())), preferred_element_type=jnp.float32
    )


def tap_inputs(tokens, device_reach):
    earlier = shifted(tokens, ("seqhi", "seqlo"), device_reach)
    later = shifted(tokens, ("seqhi", "seqlo"), -device_reach)
    return (earlier, tokens, later)


def residual_block_forward(tokens, conv_weight, proj_weight, device_reach):
    width = tokens.shape[1]
    tap_rows = tap_inputs(tokens, device_reach)
    pre = jnp.dot(tokens, conv_weight[width : 2 * width], preferred_element_type=jnp.float32)
    pre = pre + jnp.dot(tap_rows[0], conv_weight[0:width], preferred_element_type=jnp.float32)
    pre = pre + jnp.dot(
        tap_rows[2], conv_weight[2 * width : 3 * width], preferred_element_type=jnp.float32
    )
    inner = jax.nn.gelu(pre).astype(jnp.bfloat16)
    mixed = lax.dot_general(
        inner, proj_weight, (((1,), (1,)), ((), ())), preferred_element_type=jnp.float32
    )
    result = (tokens.astype(jnp.float32) + mixed).astype(jnp.bfloat16)
    return (result, tap_rows, pre, inner)


def reduce_terms(grad_terms):
    outer_count = lax.axis_size("seqhi")
    inner_count = lax.axis_size("seqlo")
    reordered = []
    for member in grad_terms:
        total_rows = member.shape[0]
        blocked = member.reshape(
            outer_count, inner_count, total_rows // (outer_count * inner_count), member.shape[1]
        )
        reordered.append(jnp.transpose(blocked, (1, 0, 2, 3)).reshape(total_rows, member.shape[1]))
    partial_sums = (
        lax.psum_scatter(
            reordered[0].astype(jnp.bfloat16), "seqlo", scatter_dimension=0, tiled=True
        ).astype(jnp.float32),
        lax.psum_scatter(
            reordered[1].astype(jnp.bfloat16), "seqlo", scatter_dimension=0, tiled=True
        ).astype(jnp.float32),
    )
    return (
        lax.psum_scatter(
            partial_sums[0].astype(jnp.bfloat16), "seqhi", scatter_dimension=0, tiled=True
        ).astype(jnp.float32),
        lax.psum_scatter(
            partial_sums[1].astype(jnp.bfloat16), "seqhi", scatter_dimension=0, tiled=True
        ).astype(jnp.float32),
    )


def residual_block_backward(grad_out, tap_rows, pre, inner, conv_weight, proj_weight, device_reach):
    width = grad_out.shape[1]
    grad_proj_term = contract_rows(grad_out, inner)
    grad_inner = jnp.dot(grad_out, proj_weight, preferred_element_type=jnp.float32)
    _, pullback = jax.vjp(jax.nn.gelu, pre)
    grad_pre = pullback(grad_inner)[0].astype(jnp.bfloat16)
    later = shifted(grad_pre, ("seqhi", "seqlo"), -device_reach)
    earlier = shifted(grad_pre, ("seqhi", "seqlo"), device_reach)
    grad_conv_term = jnp.concatenate(
        [contract_rows(tap_rows[tap_index], grad_pre) for tap_index in range(3)], 0
    )
    grad_in = grad_out.astype(jnp.float32)
    moved = (later, grad_pre, earlier)
    for tap_index in range(3):
        grad_in = grad_in + lax.dot_general(
            moved[tap_index],
            conv_weight[tap_index * width : (tap_index + 1) * width],
            (((1,), (1,)), ((), ())),
            preferred_element_type=jnp.float32,
        )
    grad_conv, grad_proj = reduce_terms((grad_conv_term, grad_proj_term))
    return (grad_in.astype(jnp.bfloat16), grad_conv, grad_proj)


def per_device_halo(
    tokens,
    cotangent,
    first_kernel_weight,
    first_pointwise_weight,
    second_kernel_weight,
    second_pointwise_weight,
):
    shard_row_block = tokens.shape[0]
    first_halo_span = FIRST_SPACING // shard_row_block
    second_halo_span = SECOND_SPACING // shard_row_block
    between_blocks_state, rows_first, first_preactivation, first_hidden_state = (
        residual_block_forward(tokens, first_kernel_weight, first_pointwise_weight, first_halo_span)
    )
    output, rows_second, second_preactivation, second_hidden_state = residual_block_forward(
        between_blocks_state, second_kernel_weight, second_pointwise_weight, second_halo_span
    )
    between_blocks_gradient, second_kernel_gradient, second_pointwise_gradient = (
        residual_block_backward(
            cotangent,
            rows_second,
            second_preactivation,
            second_hidden_state,
            second_kernel_weight,
            second_pointwise_weight,
            second_halo_span,
        )
    )
    token_rows_gradient, first_kernel_gradient, first_pointwise_gradient = residual_block_backward(
        between_blocks_gradient,
        rows_first,
        first_preactivation,
        first_hidden_state,
        first_kernel_weight,
        first_pointwise_weight,
        first_halo_span,
    )
    return (
        output,
        token_rows_gradient,
        first_kernel_gradient,
        first_pointwise_gradient,
        second_kernel_gradient,
        second_pointwise_gradient,
    )


def local_shift(values, by):
    padding = jnp.zeros((abs(by), values.shape[1]), values.dtype)
    if by > 0:
        return jnp.concatenate([padding, values[:-by]], 0)
    return jnp.concatenate([values[-by:], padding], 0)


def local_forward(x, conv, proj, step):
    width = x.shape[1]
    taps = (local_shift(x, step), x, local_shift(x, -step))
    pre = sum(
        jnp.dot(taps[k], conv[k * width : (k + 1) * width], preferred_element_type=jnp.float32)
        for k in range(3)
    )
    inner = jax.nn.gelu(pre).astype(jnp.bfloat16)
    mixed = lax.dot_general(inner, proj, (((1,), (1,)), ((), ())), preferred_element_type=jnp.float32)
    return (x.astype(jnp.float32) + mixed).astype(jnp.bfloat16), pre, inner


def local_backward(g, x, pre, inner, conv, proj, step):
    width = g.shape[1]
    grad_proj = contract_rows(g, inner)
    _, pullback = jax.vjp(jax.nn.gelu, pre)
    grad_pre = pullback(jnp.dot(g, proj, preferred_element_type=jnp.float32))[0].astype(jnp.bfloat16)
    moved = (local_shift(grad_pre, -step), grad_pre, local_shift(grad_pre, step))
    grad_conv = jnp.concatenate([contract_rows(x, m) for m in moved], 0)
    gx = g.astype(jnp.float32)
    for k in range(3):
        gx = gx + lax.dot_general(
            moved[k], conv[k * width : (k + 1) * width], (((1,), (1,)), ((), ())),
            preferred_element_type=jnp.float32,
        )
    return gx.astype(jnp.bfloat16), grad_conv, grad_proj


def per_device(tokens, cotangent, c1, p1, c2, p2):
    outer = lax.axis_size("seqhi")
    inner_count = lax.axis_size("seqlo")
    rows = tokens.shape[0]
    if rows * inner_count != FIRST_SPACING or rows % outer:
        return per_device_halo(tokens, cotangent, c1, p1, c2, p2)
    part = rows // outer
    exchange = lambda a: lax.all_to_all(a, "seqhi", 0, 0, tiled=True)
    x = exchange(tokens)
    g = exchange(cotangent)
    mid, pre1, inner1 = local_forward(x, c1, p1, part)
    out, pre2, inner2 = local_forward(mid, c2, p2, part * (SECOND_SPACING // FIRST_SPACING))
    gmid, gc2, gp2 = local_backward(g, mid, pre2, inner2, c2, p2, part * (SECOND_SPACING // FIRST_SPACING))
    gx, gc1, gp1 = local_backward(gmid, x, pre1, inner1, c1, p1, part)
    gc2, gp2 = reduce_terms((gc2, gp2))
    gc1, gp1 = reduce_terms((gc1, gp1))
    return exchange(out), exchange(gx), gc1, gp1, gc2, gp2


def solution(mesh):
    placed = (P(("seqhi", "seqlo"), None), P(("seqhi", "seqlo"), None), P(), P(), P(), P())
    return jax.shard_map(
        per_device,
        mesh=mesh,
        in_specs=placed,
        out_specs=(
            P(("seqhi", "seqlo"), None),
            P(("seqhi", "seqlo"), None),
            P(("seqhi", "seqlo"), None),
            P(("seqhi", "seqlo"), None),
            P(("seqhi", "seqlo"), None),
            P(("seqhi", "seqlo"), None),
        ),
        check_vma=False,
    )
```

```python
import functools
import math

import jax
import jax.numpy as jnp
from jax import lax
from jax.experimental import pallas as pl
from jax.experimental.pallas import tpu as pltpu
from jax.sharding import PartitionSpec as P

FIRST_SPACING = 4096
SECOND_SPACING = 8192


def shifted(x, axis, by):
    devices = lax.axis_size(axis)
    pairs = [(i, i + by) for i in range(devices) if 0 <= i + by < devices]
    return lax.ppermute(x, axis, pairs)


def contract_rows(left, right):
    return lax.dot_general(
        left, right, (((0,), (0,)), ((), ())), preferred_element_type=jnp.float32
    )


def tap_inputs(tokens, device_reach):
    earlier = shifted(tokens, ("seqhi", "seqlo"), device_reach)
    later = shifted(tokens, ("seqhi", "seqlo"), -device_reach)
    return (earlier, tokens, later)


def residual_block_forward(tokens, conv_weight, proj_weight, device_reach):
    width = tokens.shape[1]
    tap_rows = tap_inputs(tokens, device_reach)
    pre = jnp.dot(tokens, conv_weight[width : 2 * width], preferred_element_type=jnp.float32)
    pre = pre + jnp.dot(tap_rows[0], conv_weight[0:width], preferred_element_type=jnp.float32)
    pre = pre + jnp.dot(
        tap_rows[2], conv_weight[2 * width : 3 * width], preferred_element_type=jnp.float32
    )
    inner = jax.nn.gelu(pre).astype(jnp.bfloat16)
    mixed = lax.dot_general(
        inner, proj_weight, (((1,), (1,)), ((), ())), preferred_element_type=jnp.float32
    )
    result = (tokens.astype(jnp.float32) + mixed).astype(jnp.bfloat16)
    return (result, tap_rows, pre, inner)


def reduce_terms(grad_terms):
    outer_count = lax.axis_size("seqhi")
    inner_count = lax.axis_size("seqlo")
    reordered = []
    for member in grad_terms:
        total_rows = member.shape[0]
        blocked = member.reshape(
            outer_count, inner_count, total_rows // (outer_count * inner_count), member.shape[1]
        )
        reordered.append(jnp.transpose(blocked, (1, 0, 2, 3)).reshape(total_rows, member.shape[1]))
    partial_sums = (
        lax.psum_scatter(
            reordered[0].astype(jnp.bfloat16), "seqlo", scatter_dimension=0, tiled=True
        ).astype(jnp.float32),
        lax.psum_scatter(
            reordered[1].astype(jnp.bfloat16), "seqlo", scatter_dimension=0, tiled=True
        ).astype(jnp.float32),
    )
    return (
        lax.psum_scatter(
            partial_sums[0].astype(jnp.bfloat16), "seqhi", scatter_dimension=0, tiled=True
        ).astype(jnp.float32),
        lax.psum_scatter(
            partial_sums[1].astype(jnp.bfloat16), "seqhi", scatter_dimension=0, tiled=True
        ).astype(jnp.float32),
    )


def residual_block_backward(grad_out, tap_rows, pre, inner, conv_weight, proj_weight, device_reach):
    width = grad_out.shape[1]
    grad_proj_term = contract_rows(grad_out, inner)
    grad_inner = jnp.dot(grad_out, proj_weight, preferred_element_type=jnp.float32)
    _, pullback = jax.vjp(jax.nn.gelu, pre)
    grad_pre = pullback(grad_inner)[0].astype(jnp.bfloat16)
    later = shifted(grad_pre, ("seqhi", "seqlo"), -device_reach)
    earlier = shifted(grad_pre, ("seqhi", "seqlo"), device_reach)
    grad_conv_term = jnp.concatenate(
        [contract_rows(tap_rows[tap_index], grad_pre) for tap_index in range(3)], 0
    )
    grad_in = grad_out.astype(jnp.float32)
    moved = (later, grad_pre, earlier)
    for tap_index in range(3):
        grad_in = grad_in + lax.dot_general(
            moved[tap_index],
            conv_weight[tap_index * width : (tap_index + 1) * width],
            (((1,), (1,)), ((), ())),
            preferred_element_type=jnp.float32,
        )
    grad_conv, grad_proj = reduce_terms((grad_conv_term, grad_proj_term))
    return (grad_in.astype(jnp.bfloat16), grad_conv, grad_proj)


def per_device_halo(
    tokens,
    cotangent,
    first_kernel_weight,
    first_pointwise_weight,
    second_kernel_weight,
    second_pointwise_weight,
):
    shard_row_block = tokens.shape[0]
    first_halo_span = FIRST_SPACING // shard_row_block
    second_halo_span = SECOND_SPACING // shard_row_block
    between_blocks_state, rows_first, first_preactivation, first_hidden_state = (
        residual_block_forward(tokens, first_kernel_weight, first_pointwise_weight, first_halo_span)
    )
    output, rows_second, second_preactivation, second_hidden_state = residual_block_forward(
        between_blocks_state, second_kernel_weight, second_pointwise_weight, second_halo_span
    )
    between_blocks_gradient, second_kernel_gradient, second_pointwise_gradient = (
        residual_block_backward(
            cotangent,
            rows_second,
            second_preactivation,
            second_hidden_state,
            second_kernel_weight,
            second_pointwise_weight,
            second_halo_span,
        )
    )
    token_rows_gradient, first_kernel_gradient, first_pointwise_gradient = residual_block_backward(
        between_blocks_gradient,
        rows_first,
        first_preactivation,
        first_hidden_state,
        first_kernel_weight,
        first_pointwise_weight,
        first_halo_span,
    )
    return (
        output,
        token_rows_gradient,
        first_kernel_gradient,
        first_pointwise_gradient,
        second_kernel_gradient,
        second_pointwise_gradient,
    )


CHUNKS = 4
MESH = pl.DeviceIdType.MESH
F32 = jnp.float32
BF16 = jnp.bfloat16
WEIGHT = {"y": 16, "x": 8, "c": 4, "z1": 2, "z0": 1}
ORDERS = (("c", "z0", "z1", "x", "y"), ("c", "x", "y", "z0", "z1"))


def gelu_pair(v):
    scale = math.sqrt(2.0 / math.pi)
    square = v * v
    t = jnp.tanh(scale * v * (1.0 + 0.044715 * square))
    half = 0.5 * (1.0 + t)
    slope = half + 0.5 * v * (1.0 - t * t) * (scale * (1.0 + 3 * 0.044715 * square))
    return v * half, slope


def moved_down(a, by):
    return jnp.concatenate([jnp.zeros((by, a.shape[1]), a.dtype), a[: a.shape[0] - by]], 0)


def moved_up(a, by):
    return jnp.concatenate([a[by:], jnp.zeros((by, a.shape[1]), a.dtype)], 0)


def nt(a, b):
    return lax.dot_general(a, b, (((1,), (1,)), ((), ())), preferred_element_type=F32)


def tn(a, b):
    return lax.dot_general(a, b, (((0,), (0,)), ((), ())), preferred_element_type=F32)


def mega(
    n, part, steps,
    tok, cot, c1, p1, c2, p2,
    out, gx, gc1, gp1, gc2, gp2,
    xs, gs, os, gxs, w1, q1, w2, q2, mid_s, in1, in2, d1, d2, ac1, ap1, ac2, ap2,
    b0s, b0r, b1s, b1r, b2s, b2r, b3s, b3r, b4s, b4r,
    ssem, rsem, lsem, wsem, zs, zr,
):
    me = lax.axis_index("seqhi")
    lo = lax.axis_index("seqlo")
    q = part // CHUNKS
    width = tok.shape[1]
    inner = w1.shape[1] // 3
    rows = n * q

    loads = []
    for k in range(3):
        for b, (src, dst) in enumerate(((c1, w1), (c2, w2))):
            loads.append(pltpu.make_async_copy(
                src.at[pl.ds(k * width, width), :],
                dst.at[:, pl.ds(k * inner, inner)], wsem.at[2 * k + b]))
    loads.append(pltpu.make_async_copy(p1, q1, wsem.at[6]))
    loads.append(pltpu.make_async_copy(p2, q2, wsem.at[7]))
    for load in loads:
        load.start()

    barrier = pltpu.get_barrier_semaphore()

    def greet(d, carry):
        pl.semaphore_signal(barrier, inc=1, device_id=(lax.rem(me + d, n), lo), device_id_type=MESH)
        return carry

    lax.fori_loop(1, n, greet, 0)
    z0, z1 = lax.rem(lo, 2), lo // 2
    near, far = lo + 1 - 2 * z0, lo + 2 - 4 * z1
    pl.semaphore_signal(barrier, inc=1, device_id=(me, near), device_id_type=MESH)
    pl.semaphore_signal(barrier, inc=1, device_id=(me, far), device_id_type=MESH)
    pl.semaphore_wait(barrier, n + 1)

    def span(owner, c):
        return pl.ds(pl.multiple_of(owner * part + c * q, 16), q)

    def inbound(a, c, peer, slot):
        src, dst = ((tok, xs), (cot, gs))[a]
        return pltpu.make_async_remote_copy(
            src_ref=src.at[span(peer, c), :], dst_ref=dst.at[c, slot],
            send_sem=ssem.at[a, c, peer], recv_sem=rsem.at[a, c, slot],
            device_id=(peer, lo), device_id_type=MESH)

    def outbound(a, c, peer, owner):
        src, dst = ((os, out), (gxs, gx))[a]
        return pltpu.make_async_remote_copy(
            src_ref=src.at[c, peer], dst_ref=dst.at[span(owner, c), :],
            send_sem=ssem.at[2 + a, c, peer], recv_sem=rsem.at[2 + a, c, owner],
            device_id=(peer, lo), device_id_type=MESH)

    def own_in(a, c):
        src, dst = ((tok, xs), (cot, gs))[a]
        return pltpu.make_async_copy(src.at[span(me, c), :], dst.at[c, me], lsem.at[a, c])

    def own_out(a, c):
        src, dst = ((os, out), (gxs, gx))[a]
        return pltpu.make_async_copy(src.at[c, me], dst.at[span(me, c), :], lsem.at[2 + a, c])

    def peers(body):
        def step(d, carry):
            body(lax.rem(me + d, n))
            return carry
        lax.fori_loop(1, n, step, 0)

    def send_chunk(c, carry):
        for a in range(2):
            own_in(a, c).start()
            peers(lambda peer: inbound(a, c, peer, me).start())
        return carry

    lax.fori_loop(0, CHUNKS, send_chunk, 0)
    for ref in (ac1, ap1, ac2, ap2):
        ref[...] = jnp.zeros(ref.shape, F32)
    for load in loads:
        load.wait()

    def forward(x, w, p, hid, slope, by):
        a = jnp.dot(x, w[...], preferred_element_type=F32)
        pre = a[:, inner : 2 * inner] + moved_down(a[:, :inner], by) + moved_up(a[:, 2 * inner :], by)
        value, slope[...] = gelu_pair(pre)
        hid[...] = value.astype(BF16)
        return (x.astype(F32) + nt(hid[...], p[...])).astype(BF16)

    def backward(g, x, w, p, hid, slope, by, ac, ap):
        ap[...] += tn(g, hid[...])
        grad = (jnp.dot(g, p[...], preferred_element_type=F32) * slope[...]).astype(BF16)
        moved = jnp.concatenate([moved_up(grad, by), grad, moved_down(grad, by)], 1)
        gc = tn(x, moved)
        for k in range(3):
            ac[pl.ds(k * width, width), :] += gc[:, k * inner : (k + 1) * inner]
        return (g.astype(F32) + nt(moved, w[...])).astype(BF16)

    def chunk(c, carry):
        own_in(0, c).wait()
        peers(lambda peer: inbound(0, c, peer, peer).wait_recv())
        mid_s[...] = forward(xs[c].reshape(rows, width), w1, q1, in1, d1, q)
        os[c] = forward(mid_s[...], w2, q2, in2, d2, steps * q).reshape(n, q, width)
        own_out(0, c).start()
        peers(lambda peer: outbound(0, c, peer, me).start())
        own_in(1, c).wait()
        peers(lambda peer: inbound(1, c, peer, peer).wait_recv())
        gmid = backward(gs[c].reshape(rows, width), mid_s[...], w2, q2, in2, d2, steps * q, ac2, ap2)
        gxs[c] = backward(gmid, xs[c].reshape(rows, width), w1, q1, in1, d1, q, ac1, ap1).reshape(n, q, width)
        own_out(1, c).start()
        peers(lambda peer: outbound(1, c, peer, me).start())
        return carry

    lax.fori_loop(0, CHUNKS, chunk, 0)

    bit = {"c": lax.rem(me, 2), "x": lax.rem(me // 2, 2), "y": me // 4, "z0": z0, "z1": z1}
    hop = {"c": 1, "x": 2, "y": 4}
    partner = {name: (me + hop[name] - 2 * hop[name] * bit[name], lo) for name in hop}
    partner["z0"], partner["z1"] = (me, near), (me, far)
    sums = ((ac2, ap2), (ac1, ap1))
    sends, recvs = (b0s, b1s, b2s, b3s, b4s), (b0r, b1r, b2r, b3r, b4r)
    cr, pr = ac1.shape[0] // 32, ap1.shape[0] // 32

    def piece(b, p):
        conv, proj = sums[b]
        return conv.at[pl.ds(pl.multiple_of(p * cr, 8), cr), :], proj.at[pl.ds(pl.multiple_of(p * pr, 8), pr), :]

    def address(b, s, m, flip):
        order = ORDERS[b]
        p = 0
        for t, name in enumerate(order):
            w = WEIGHT[name]
            if t < s:
                p = p + bit[name] * w
            elif t == s:
                p = p + ((1 - bit[name]) if flip else bit[name]) * w
            else:
                p = p + lax.rem(m // (1 << (4 - t)), 2) * w
        return p

    def exchange(b, s):
        return pltpu.make_async_remote_copy(
            src_ref=sends[s].at[b], dst_ref=recvs[s].at[b], send_sem=zs.at[b, s], recv_sem=zr.at[b, s],
            device_id=partner[ORDERS[b][s]], device_id_type=MESH)

    def arrived(b, s, m, flip):
        got = recvs[s - 1][b, ((1 - bit[ORDERS[b][s]]) if flip else bit[ORDERS[b][s]]) * (1 << (4 - s)) + m]
        return got.astype(F32)

    for s in range(5):
        count = 1 << (4 - s)
        for b in range(2):
            if s:
                exchange(b, s - 1).wait_recv()

            def give(m, carry):
                conv, proj = piece(b, address(b, s, m, True))
                value = jnp.concatenate([conv[...], proj[...]], 0)
                if s:
                    value = value + arrived(b, s, m, True)
                sends[s][b, m] = value.astype(BF16)
                return carry

            lax.fori_loop(0, count, give, 0)
            exchange(b, s).start()
        if s:
            for b in range(2):
                def keep(m, carry):
                    conv, proj = piece(b, address(b, s, m, False))
                    got = arrived(b, s, m, False)
                    conv[...] += got[:cr]
                    proj[...] += got[cr:]
                    return carry

                lax.fori_loop(0, count, keep, 0)
    for b, (conv_out, proj_out) in enumerate(((gc2, gp2), (gc1, gp1))):
        exchange(b, 4).wait_recv()
        conv, proj = piece(b, address(b, 5, 0, False))
        got = recvs[4][b, 0].astype(F32)
        conv_out[...] = conv[...] + got[:cr]
        proj_out[...] = proj[...] + got[cr:]
        for s in range(5):
            exchange(b, s).wait_send()

    def drain(c, carry):
        for a in range(2):
            own_out(a, c).wait()
            peers(lambda peer: inbound(a, c, peer, me).wait_send())
            peers(lambda peer: outbound(a, c, peer, me).wait_send())
            peers(lambda peer: outbound(a, c, peer, peer).wait_recv())
        return carry

    lax.fori_loop(0, CHUNKS, drain, 0)


def per_device(tokens, cotangent, c1, p1, c2, p2):
    n = lax.axis_size("seqhi")
    inner_count = lax.axis_size("seqlo")
    rows, width = tokens.shape
    inner = p1.shape[1]
    pieces = n * inner_count
    if rows * inner_count != FIRST_SPACING or (n, inner_count) != (8, 4) or rows % (n * CHUNKS * 16):
        return per_device_halo(tokens, cotangent, c1, p1, c2, p2)
    part = rows // n
    q = part // CHUNKS
    slots = pltpu.VMEM((CHUNKS, n, q, width), BF16)
    tile = (c1.shape[0] + p1.shape[0]) // pieces
    scratch = [slots] * 4
    scratch += [pltpu.VMEM((width, 3 * inner), BF16), pltpu.VMEM((width, inner), BF16)] * 2
    scratch += [pltpu.VMEM((n * q, width), BF16)]
    scratch += [pltpu.VMEM((n * q, inner), BF16)] * 2 + [pltpu.VMEM((n * q, inner), F32)] * 2
    scratch += [pltpu.VMEM(c1.shape, F32), pltpu.VMEM(p1.shape, F32)] * 2
    for s in range(5):
        scratch += [pltpu.VMEM((2, 1 << (4 - s), tile, inner), BF16)] * 2
    scratch += [pltpu.SemaphoreType.DMA((4, CHUNKS, n))] * 2
    scratch += [pltpu.SemaphoreType.DMA((4, CHUNKS)), pltpu.SemaphoreType.DMA((8,))]
    scratch += [pltpu.SemaphoreType.DMA((2, 5))] * 2
    grads = [(a.shape[0] // pieces, inner) for a in (c1, p1, c2, p2)]
    return pl.pallas_call(
        functools.partial(mega, n, part, SECOND_SPACING // FIRST_SPACING),
        out_shape=[jax.ShapeDtypeStruct(tokens.shape, BF16)] * 2
        + [jax.ShapeDtypeStruct(g, F32) for g in grads],
        in_specs=[pl.BlockSpec(memory_space=pl.ANY)] * 6,
        out_specs=[pl.BlockSpec(memory_space=pl.ANY)] * 2 + [pl.BlockSpec(memory_space=pltpu.VMEM)] * 4,
        scratch_shapes=scratch,
        compiler_params=pltpu.CompilerParams(
            collective_id=0, has_side_effects=True, vmem_limit_bytes=60 * 1024 * 1024),
    )(tokens, cotangent, c1, p1, c2, p2)


def solution(mesh):
    placed = (P(("seqhi", "seqlo"), None), P(("seqhi", "seqlo"), None), P(), P(), P(), P())
    return jax.shard_map(
        per_device,
        mesh=mesh,
        in_specs=placed,
        out_specs=(
            P(("seqhi", "seqlo"), None),
            P(("seqhi", "seqlo"), None),
            P(("seqhi", "seqlo"), None),
            P(("seqhi", "seqlo"), None),
            P(("seqhi", "seqlo"), None),
            P(("seqhi", "seqlo"), None),
        ),
        check_vma=False,
    )
```

```python
import functools
import math

import jax
import jax.numpy as jnp
from jax import lax
from jax.experimental import pallas as pl
from jax.experimental.pallas import tpu as pltpu
from jax.sharding import PartitionSpec as P

FIRST_SPACING = 4096
SECOND_SPACING = 8192


def shifted(x, axis, by):
    devices = lax.axis_size(axis)
    pairs = [(i, i + by) for i in range(devices) if 0 <= i + by < devices]
    return lax.ppermute(x, axis, pairs)


def contract_rows(left, right):
    return lax.dot_general(
        left, right, (((0,), (0,)), ((), ())), preferred_element_type=jnp.float32
    )


def tap_inputs(tokens, device_reach):
    earlier = shifted(tokens, ("seqhi", "seqlo"), device_reach)
    later = shifted(tokens, ("seqhi", "seqlo"), -device_reach)
    return (earlier, tokens, later)


def residual_block_forward(tokens, conv_weight, proj_weight, device_reach):
    width = tokens.shape[1]
    tap_rows = tap_inputs(tokens, device_reach)
    pre = jnp.dot(tokens, conv_weight[width : 2 * width], preferred_element_type=jnp.float32)
    pre = pre + jnp.dot(tap_rows[0], conv_weight[0:width], preferred_element_type=jnp.float32)
    pre = pre + jnp.dot(
        tap_rows[2], conv_weight[2 * width : 3 * width], preferred_element_type=jnp.float32
    )
    inner = jax.nn.gelu(pre).astype(jnp.bfloat16)
    mixed = lax.dot_general(
        inner, proj_weight, (((1,), (1,)), ((), ())), preferred_element_type=jnp.float32
    )
    result = (tokens.astype(jnp.float32) + mixed).astype(jnp.bfloat16)
    return (result, tap_rows, pre, inner)


def reduce_terms(grad_terms):
    outer_count = lax.axis_size("seqhi")
    inner_count = lax.axis_size("seqlo")
    reordered = []
    for member in grad_terms:
        total_rows = member.shape[0]
        blocked = member.reshape(
            outer_count, inner_count, total_rows // (outer_count * inner_count), member.shape[1]
        )
        reordered.append(jnp.transpose(blocked, (1, 0, 2, 3)).reshape(total_rows, member.shape[1]))
    partial_sums = (
        lax.psum_scatter(
            reordered[0].astype(jnp.bfloat16), "seqlo", scatter_dimension=0, tiled=True
        ).astype(jnp.float32),
        lax.psum_scatter(
            reordered[1].astype(jnp.bfloat16), "seqlo", scatter_dimension=0, tiled=True
        ).astype(jnp.float32),
    )
    return (
        lax.psum_scatter(
            partial_sums[0].astype(jnp.bfloat16), "seqhi", scatter_dimension=0, tiled=True
        ).astype(jnp.float32),
        lax.psum_scatter(
            partial_sums[1].astype(jnp.bfloat16), "seqhi", scatter_dimension=0, tiled=True
        ).astype(jnp.float32),
    )


def residual_block_backward(grad_out, tap_rows, pre, inner, conv_weight, proj_weight, device_reach):
    width = grad_out.shape[1]
    grad_proj_term = contract_rows(grad_out, inner)
    grad_inner = jnp.dot(grad_out, proj_weight, preferred_element_type=jnp.float32)
    _, pullback = jax.vjp(jax.nn.gelu, pre)
    grad_pre = pullback(grad_inner)[0].astype(jnp.bfloat16)
    later = shifted(grad_pre, ("seqhi", "seqlo"), -device_reach)
    earlier = shifted(grad_pre, ("seqhi", "seqlo"), device_reach)
    grad_conv_term = jnp.concatenate(
        [contract_rows(tap_rows[tap_index], grad_pre) for tap_index in range(3)], 0
    )
    grad_in = grad_out.astype(jnp.float32)
    moved = (later, grad_pre, earlier)
    for tap_index in range(3):
        grad_in = grad_in + lax.dot_general(
            moved[tap_index],
            conv_weight[tap_index * width : (tap_index + 1) * width],
            (((1,), (1,)), ((), ())),
            preferred_element_type=jnp.float32,
        )
    grad_conv, grad_proj = reduce_terms((grad_conv_term, grad_proj_term))
    return (grad_in.astype(jnp.bfloat16), grad_conv, grad_proj)


def per_device_halo(
    tokens,
    cotangent,
    first_kernel_weight,
    first_pointwise_weight,
    second_kernel_weight,
    second_pointwise_weight,
):
    shard_row_block = tokens.shape[0]
    first_halo_span = FIRST_SPACING // shard_row_block
    second_halo_span = SECOND_SPACING // shard_row_block
    between_blocks_state, rows_first, first_preactivation, first_hidden_state = (
        residual_block_forward(tokens, first_kernel_weight, first_pointwise_weight, first_halo_span)
    )
    output, rows_second, second_preactivation, second_hidden_state = residual_block_forward(
        between_blocks_state, second_kernel_weight, second_pointwise_weight, second_halo_span
    )
    between_blocks_gradient, second_kernel_gradient, second_pointwise_gradient = (
        residual_block_backward(
            cotangent,
            rows_second,
            second_preactivation,
            second_hidden_state,
            second_kernel_weight,
            second_pointwise_weight,
            second_halo_span,
        )
    )
    token_rows_gradient, first_kernel_gradient, first_pointwise_gradient = residual_block_backward(
        between_blocks_gradient,
        rows_first,
        first_preactivation,
        first_hidden_state,
        first_kernel_weight,
        first_pointwise_weight,
        first_halo_span,
    )
    return (
        output,
        token_rows_gradient,
        first_kernel_gradient,
        first_pointwise_gradient,
        second_kernel_gradient,
        second_pointwise_gradient,
    )


CHUNKS = 4
AT_ONCE = 2
LATE = {1: (2,), 2: (3,)}
MESH = pl.DeviceIdType.MESH
F32 = jnp.float32
BF16 = jnp.bfloat16
WEIGHT = {"y": 16, "x": 8, "c": 4, "z1": 2, "z0": 1}
ORDERS = (("c", "z0", "z1", "x", "y"), ("c", "x", "y", "z0", "z1"))


def gelu_pair(v):
    scale = math.sqrt(2.0 / math.pi)
    square = v * v
    t = jnp.tanh(scale * v * (1.0 + 0.044715 * square))
    half = 0.5 * (1.0 + t)
    slope = half + 0.5 * v * (1.0 - t * t) * (scale * (1.0 + 3 * 0.044715 * square))
    return v * half, slope


def moved_down(a, by):
    return jnp.concatenate([jnp.zeros((by, a.shape[1]), a.dtype), a[: a.shape[0] - by]], 0)


def moved_up(a, by):
    return jnp.concatenate([a[by:], jnp.zeros((by, a.shape[1]), a.dtype)], 0)


def nt(a, b):
    return lax.dot_general(a, b, (((1,), (1,)), ((), ())), preferred_element_type=F32)


def tn(a, b):
    return lax.dot_general(a, b, (((0,), (0,)), ((), ())), preferred_element_type=F32)


def mega(
    n, part, steps,
    tok, cot, c1, p1, c2, p2,
    out, gx, gc1, gp1, gc2, gp2,
    xs, gs, os, gxs, w1, q1, w2, q2, mid_s, in1, in2, d1, d2, ac1, ap1, ac2, ap2,
    b0s, b0r, b1s, b1r, b2s, b2r, b3s, b3r, b4s, b4r,
    ssem, rsem, lsem, wsem, zs, zr,
):
    me = lax.axis_index("seqhi")
    lo = lax.axis_index("seqlo")
    q = part // CHUNKS
    width = tok.shape[1]
    inner = w1.shape[1] // 3
    rows = n * q

    loads = []
    for k in range(3):
        for b, (src, dst) in enumerate(((c1, w1), (c2, w2))):
            loads.append(pltpu.make_async_copy(
                src.at[pl.ds(k * width, width), :],
                dst.at[:, pl.ds(k * inner, inner)], wsem.at[2 * k + b]))
    loads.append(pltpu.make_async_copy(p1, q1, wsem.at[6]))
    loads.append(pltpu.make_async_copy(p2, q2, wsem.at[7]))
    for load in loads:
        load.start()

    barrier = pltpu.get_barrier_semaphore()

    def greet(d, carry):
        pl.semaphore_signal(barrier, inc=1, device_id=(lax.rem(me + d, n), lo), device_id_type=MESH)
        return carry

    lax.fori_loop(1, n, greet, 0)
    z0, z1 = lax.rem(lo, 2), lo // 2
    near, far = lo + 1 - 2 * z0, lo + 2 - 4 * z1
    pl.semaphore_signal(barrier, inc=1, device_id=(me, near), device_id_type=MESH)
    pl.semaphore_signal(barrier, inc=1, device_id=(me, far), device_id_type=MESH)
    pl.semaphore_wait(barrier, n + 1)

    def span(owner, c):
        return pl.ds(pl.multiple_of(owner * part + c * q, 16), q)

    def inbound(a, c, peer, slot):
        src, dst = ((tok, xs), (cot, gs))[a]
        return pltpu.make_async_remote_copy(
            src_ref=src.at[span(peer, c), :], dst_ref=dst.at[c, slot],
            send_sem=ssem.at[a, c, peer], recv_sem=rsem.at[a, c, slot],
            device_id=(peer, lo), device_id_type=MESH)

    def outbound(a, c, peer, owner):
        src, dst = ((os, out), (gxs, gx))[a]
        return pltpu.make_async_remote_copy(
            src_ref=src.at[c, peer], dst_ref=dst.at[span(owner, c), :],
            send_sem=ssem.at[2 + a, c, peer], recv_sem=rsem.at[2 + a, c, owner],
            device_id=(peer, lo), device_id_type=MESH)

    def own_in(a, c):
        src, dst = ((tok, xs), (cot, gs))[a]
        return pltpu.make_async_copy(src.at[span(me, c), :], dst.at[c, me], lsem.at[a, c])

    def own_out(a, c):
        src, dst = ((os, out), (gxs, gx))[a]
        return pltpu.make_async_copy(src.at[c, me], dst.at[span(me, c), :], lsem.at[2 + a, c])

    def peers(body):
        def step(i, carry):
            body(lax.rem(me + i, n))
            return carry
        lax.fori_loop(1, n, step, 0)

    def send_chunk(c, carry):
        for a in range(2):
            own_in(a, c).start()
            peers(lambda peer: inbound(a, c, peer, me).start())
        return carry

    lax.fori_loop(0, CHUNKS, send_chunk, 0)
    for ref in (ac1, ap1, ac2, ap2):
        ref[...] = jnp.zeros(ref.shape, F32)
    for load in loads:
        load.wait()

    def forward(x, w, p, hid, slope, by):
        a = jnp.dot(x, w[...], preferred_element_type=F32)
        pre = a[:, inner : 2 * inner] + moved_down(a[:, :inner], by) + moved_up(a[:, 2 * inner :], by)
        value, slope[...] = gelu_pair(pre)
        hid[...] = value.astype(BF16)
        return (x.astype(F32) + nt(hid[...], p[...])).astype(BF16)

    def backward(g, x, w, p, hid, slope, by, ac, ap):
        ap[...] += tn(g, hid[...])
        grad = (jnp.dot(g, p[...], preferred_element_type=F32) * slope[...]).astype(BF16)
        moved = jnp.concatenate([moved_up(grad, by), grad, moved_down(grad, by)], 1)
        gc = tn(x, moved)
        for k in range(3):
            ac[pl.ds(k * width, width), :] += gc[:, k * inner : (k + 1) * inner]
        return (g.astype(F32) + nt(moved, w[...])).astype(BF16)

    def ship(a, c):
        own_out(a, c).start()
        peers(lambda peer: outbound(a, c, peer, me).start())

    def chunk(c, carry):
        own_in(0, c).wait()
        peers(lambda peer: inbound(0, c, peer, peer).wait_recv())
        mid_s[...] = forward(xs[c].reshape(rows, width), w1, q1, in1, d1, q)
        os[c] = forward(mid_s[...], w2, q2, in2, d2, steps * q).reshape(n, q, width)
        pl.when(c < AT_ONCE)(lambda: ship(0, c))
        own_in(1, c).wait()
        peers(lambda peer: inbound(1, c, peer, peer).wait_recv())
        gmid = backward(gs[c].reshape(rows, width), mid_s[...], w2, q2, in2, d2, steps * q, ac2, ap2)
        gxs[c] = backward(gmid, xs[c].reshape(rows, width), w1, q1, in1, d1, q, ac1, ap1).reshape(n, q, width)
        pl.when(c < AT_ONCE)(lambda: ship(1, c))
        return carry

    lax.fori_loop(0, CHUNKS, chunk, 0)

    bit = {"c": lax.rem(me, 2), "x": lax.rem(me // 2, 2), "y": me // 4, "z0": z0, "z1": z1}
    hop = {"c": 1, "x": 2, "y": 4}
    partner = {name: (me + hop[name] - 2 * hop[name] * bit[name], lo) for name in hop}
    partner["z0"], partner["z1"] = (me, near), (me, far)
    sums = ((ac2, ap2), (ac1, ap1))
    sends, recvs = (b0s, b1s, b2s, b3s, b4s), (b0r, b1r, b2r, b3r, b4r)
    cr, pr = ac1.shape[0] // 32, ap1.shape[0] // 32

    def piece(b, p):
        conv, proj = sums[b]
        return conv.at[pl.ds(pl.multiple_of(p * cr, 8), cr), :], proj.at[pl.ds(pl.multiple_of(p * pr, 8), pr), :]

    def address(b, s, m, flip):
        order = ORDERS[b]
        p = 0
        for t, name in enumerate(order):
            w = WEIGHT[name]
            if t < s:
                p = p + bit[name] * w
            elif t == s:
                p = p + ((1 - bit[name]) if flip else bit[name]) * w
            else:
                p = p + lax.rem(m // (1 << (4 - t)), 2) * w
        return p

    def exchange(b, s):
        return pltpu.make_async_remote_copy(
            src_ref=sends[s].at[b], dst_ref=recvs[s].at[b], send_sem=zs.at[b, s], recv_sem=zr.at[b, s],
            device_id=partner[ORDERS[b][s]], device_id_type=MESH)

    def arrived(b, s, m, flip):
        got = recvs[s - 1][b, ((1 - bit[ORDERS[b][s]]) if flip else bit[ORDERS[b][s]]) * (1 << (4 - s)) + m]
        return got.astype(F32)

    for s in range(5):
        count = 1 << (4 - s)
        for b in range(2):
            if s:
                exchange(b, s - 1).wait_recv()

            def give(m, carry):
                conv, proj = piece(b, address(b, s, m, True))
                value = jnp.concatenate([conv[...], proj[...]], 0)
                if s:
                    value = value + arrived(b, s, m, True)
                sends[s][b, m] = value.astype(BF16)
                return carry

            lax.fori_loop(0, count, give, 0)
            exchange(b, s).start()
        for c in LATE.get(s, ()):
            ship(0, c)
            ship(1, c)
        if s:
            for b in range(2):
                def keep(m, carry):
                    conv, proj = piece(b, address(b, s, m, False))
                    got = arrived(b, s, m, False)
                    conv[...] += got[:cr]
                    proj[...] += got[cr:]
                    return carry

                lax.fori_loop(0, count, keep, 0)
    for b, (conv_out, proj_out) in enumerate(((gc2, gp2), (gc1, gp1))):
        exchange(b, 4).wait_recv()
        conv, proj = piece(b, address(b, 5, 0, False))
        got = recvs[4][b, 0].astype(F32)
        conv_out[...] = conv[...] + got[:cr]
        proj_out[...] = proj[...] + got[cr:]
        for s in range(5):
            exchange(b, s).wait_send()

    def drain(c, carry):
        for a in range(2):
            own_out(a, c).wait()
            peers(lambda peer: inbound(a, c, peer, me).wait_send())
            peers(lambda peer: outbound(a, c, peer, me).wait_send())
            peers(lambda peer: outbound(a, c, peer, peer).wait_recv())
        return carry

    lax.fori_loop(0, CHUNKS, drain, 0)


def per_device(tokens, cotangent, c1, p1, c2, p2):
    n = lax.axis_size("seqhi")
    inner_count = lax.axis_size("seqlo")
    rows, width = tokens.shape
    inner = p1.shape[1]
    pieces = n * inner_count
    if rows * inner_count != FIRST_SPACING or (n, inner_count) != (8, 4) or rows % (n * CHUNKS * 16):
        return per_device_halo(tokens, cotangent, c1, p1, c2, p2)
    part = rows // n
    q = part // CHUNKS
    slots = pltpu.VMEM((CHUNKS, n, q, width), BF16)
    tile = (c1.shape[0] + p1.shape[0]) // pieces
    scratch = [slots] * 4
    scratch += [pltpu.VMEM((width, 3 * inner), BF16), pltpu.VMEM((width, inner), BF16)] * 2
    scratch += [pltpu.VMEM((n * q, width), BF16)]
    scratch += [pltpu.VMEM((n * q, inner), BF16)] * 2 + [pltpu.VMEM((n * q, inner), F32)] * 2
    scratch += [pltpu.VMEM(c1.shape, F32), pltpu.VMEM(p1.shape, F32)] * 2
    for s in range(5):
        scratch += [pltpu.VMEM((2, 1 << (4 - s), tile, inner), BF16)] * 2
    scratch += [pltpu.SemaphoreType.DMA((4, CHUNKS, n))] * 2
    scratch += [pltpu.SemaphoreType.DMA((4, CHUNKS)), pltpu.SemaphoreType.DMA((8,))]
    scratch += [pltpu.SemaphoreType.DMA((2, 5))] * 2
    grads = [(a.shape[0] // pieces, inner) for a in (c1, p1, c2, p2)]
    return pl.pallas_call(
        functools.partial(mega, n, part, SECOND_SPACING // FIRST_SPACING),
        out_shape=[jax.ShapeDtypeStruct(tokens.shape, BF16)] * 2
        + [jax.ShapeDtypeStruct(g, F32) for g in grads],
        in_specs=[pl.BlockSpec(memory_space=pl.ANY)] * 6,
        out_specs=[pl.BlockSpec(memory_space=pl.ANY)] * 2 + [pl.BlockSpec(memory_space=pltpu.VMEM)] * 4,
        scratch_shapes=scratch,
        compiler_params=pltpu.CompilerParams(
            collective_id=0, has_side_effects=True, vmem_limit_bytes=60 * 1024 * 1024),
    )(tokens, cotangent, c1, p1, c2, p2)


def solution(mesh):
    placed = (P(("seqhi", "seqlo"), None), P(("seqhi", "seqlo"), None), P(), P(), P(), P())
    return jax.shard_map(
        per_device,
        mesh=mesh,
        in_specs=placed,
        out_specs=(
            P(("seqhi", "seqlo"), None),
            P(("seqhi", "seqlo"), None),
            P(("seqhi", "seqlo"), None),
            P(("seqhi", "seqlo"), None),
            P(("seqhi", "seqlo"), None),
            P(("seqhi", "seqlo"), None),
        ),
        check_vma=False,
    )
```
